128 devices in a mesh: req: 64 (over y, z_hi, x, core), tp: 2 (over z_lo).
Axes of the slice: x: 4, y: 4, z: 4 (z_hi: 2, z_lo: 2; z = z_hi * 2 + z_lo), core: 2. Of those that a mesh axis runs over, the one named last changes fastest.
Arguments:
- tokens: bfloat16 [32768, 2048], P('req', 'tp'), may hold values from -6 to 6
- attn_gain: float32 [2048], replicated, may hold values from 0.1 to 1.9
- w_query: bfloat16 [2048, 1024], P(None, 'tp'), may hold values from -0.25 to 0.25
- key_weight: bfloat16 [2048, 256], P(None, 'tp'), may hold values from -0.125 to 0.125
- value_weight: bfloat16 [2048, 256], P(None, 'tp'), may hold values from -0.125 to 0.125
- w_attn_out: bfloat16 [1024, 2048], P('tp'), may hold values from -1 to 1
- kv_pages: bfloat16 [4096, 2, 2, 128, 128], P('req', None, 'tp'), may hold values from -240 to 240
- page_table: int32 [64, 32], P('req'), may hold values from 0 to 4095, as said below
- cached_len: int32 [64], P('req'), may hold values from 3072 to 4096, as said below
- w_gate_z: bfloat16 [2048, 1536], P(None, 'tp'), may hold values from -0.125 to 0.125
- w_ssm_in: bfloat16 [2048, 1536], P(None, 'tp'), may hold values from -0.125 to 0.125
- w_bc: bfloat16 [2048, 512], replicated, may hold values from -0.125 to 0.125
- w_dt: bfloat16 [2048, 24], P(None, 'tp'), may hold values from -0.125 to 0.125
- conv_w_x: float32 [4, 1536], P(None, 'tp'), may hold values from -3 to 3
- conv_w_bc: float32 [4, 512], replicated, may hold values from -3 to 3
- conv_x_state: bfloat16 [64, 3, 1536], P('req', None, 'tp'), may hold values from -6 to 6
- conv_bc_state: bfloat16 [64, 3, 512], P('req'), may hold values from -6 to 6
- dt_bias: float32 [24], P('tp'), may hold values from -3 to 0
- decay_rate: float32 [24], P('tp'), may hold values from 0.002 to 0.2
- skip_gain: float32 [24], P('tp'), may hold values from 0.5 to 1.5
- mixer_gain: float32 [1536], P('tp'), may hold values from 0.1 to 1.9
- w_mixer_out: bfloat16 [1536, 2048], P('tp'), may hold values from -0.15625 to 0.15625
- ssm_state: float32 [64, 24, 64, 256], P('req', 'tp'), may hold values from -6 to 6
Outputs:
- mixed: bfloat16 [32768, 2048], P('req', 'tp')
- final_state: float32 [64, 24, 64, 256], P('req', 'tp')
The draws below stay inside these ranges and needn't reach their ends.
Inputs may be any that keep to these rules, and one draw needn't show every extreme that they name: `page_table`: entries are page numbers below 4096. Of one request's 32 entries at most 1 lie among the pages of one index of req, and some request has exactly 1 there. Requests in aligned runs of 4 may share their leading entries. `cached_len`: some request has exactly 4096.
All inputs are finite; a program needn't handle non-finite values.
Results may differ from the reference program's by a relative error of at most 0.018.
The reference program's roundings to bfloat16 on the way count: a program that leaves them out, or rounds other values in their place, can miss the bound.
Values may be sent and summed in bfloat16 or wider, within the bound.
A program may use at most 128 MiB of HBM per device.

```python
import math
import jax
import jax.numpy as jnp
from jax import lax

MODEL_WIDTH = 2048
QUERY_HEADS = 8
KEY_VALUE_HEADS = 2
HEAD_SIZE = 128
MH = 24
MP = 64
MN = 256
KCONV = 4
PAGE_TOKENS = 128
TABLE_ENTRIES = 32
GROUP = 4
NEW_TOKENS = 512
REQS = 64
TOKENS = 32768
PAGES_DEV = 64
PAGE_TOTAL = 4096
MAXCTX = 4096
DSSM = 1536


def draw_lengths(key):
    spread = jax.random.randint(jax.random.fold_in(key, 11), (REQS,), 3 * MAXCTX // 4, MAXCTX + 1)
    chosen = jax.random.randint(jax.random.fold_in(key, 12), (), 0, REQS)
    return jnp.where(jnp.arange(REQS) == chosen, MAXCTX, spread).astype(jnp.int32)


def draw_cached_len(key, part):
    return draw_lengths(key)


def draw_page_table(key, part):
    lengths = draw_lengths(key)
    groups = REQS // GROUP
    capacity = PAGES_DEV // REQS
    full_pages = (lengths // PAGE_TOKENS).reshape(groups, GROUP)
    share_top = jnp.minimum(jnp.min(full_pages, axis=1), TABLE_ENTRIES - 1)
    shared = jax.random.randint(jax.random.fold_in(key, 13), (groups,), 0, share_top + 1)
    group_keys = jax.random.split(jax.random.fold_in(key, 14), groups)
    orders = jax.vmap(lambda group_key: jax.random.permutation(group_key, REQS))(group_keys).astype(jnp.int32)
    last_place = (TABLE_ENTRIES - 1) // capacity
    order_index = jnp.arange(REQS, dtype=jnp.int32)
    last_order = orders[groups - 1]
    swapped = jnp.where(last_order == REQS - 1, last_order[last_place], jnp.where(order_index == last_place, REQS - 1, last_order))
    orders = orders.at[groups - 1].set(swapped.astype(jnp.int32))
    request = jnp.arange(REQS, dtype=jnp.int32)
    page_index = jnp.arange(TABLE_ENTRIES, dtype=jnp.int32)
    group_of = request // GROUP
    owners = orders[group_of][:, page_index // capacity]
    leader = group_of * GROUP
    holder = jnp.where(page_index[None, :] < shared[group_of][:, None], leader[:, None], request[:, None])
    slot_ids = holder * capacity + page_index[None, :] % capacity
    return (owners * PAGES_DEV + slot_ids).astype(jnp.int32)


def draw_kv_pages(key, part):
    value_vectors = jnp.clip(jax.random.normal(key, (PAGE_TOTAL, 2, KEY_VALUE_HEADS, PAGE_TOKENS, HEAD_SIZE), jnp.float32), -6.0, 6.0)
    return value_vectors.astype(jnp.bfloat16)


def level_of(key, dims, cuts, smallest, top_value):
    gain, own = 1.0, jax.random.fold_in(key, 6)
    for position, parts in cuts:
        draws = jnp.exp(jax.random.uniform(jax.random.fold_in(own, position), (parts,), jnp.float32, smallest / len(cuts), top_value / len(cuts)))
        gain = gain * jnp.repeat(draws, dims[position] // parts).reshape([-1 if axis == position else 1 for axis in range(len(dims))])
    return gain


def scatter_about(key, extent, scale, limit, cuts=(), kind=jnp.bfloat16):
    values = scale * jax.random.normal(key, extent, jnp.float32)
    if cuts:
        values = values * level_of(key, extent, cuts, -0.22, 0.18)
    return jnp.clip(values, -limit, limit).astype(kind)


def setup_inputs(seed: int = 0) -> dict:
    arg_keys = jax.random.split(jax.random.key(seed), 24)
    tokens = scatter_about(arg_keys[0], (TOKENS, MODEL_WIDTH), 1.0, 6.0, ((0, 64), (1, 2)))
    attn_gain = jnp.clip(1.0 + 0.18 * jax.random.normal(arg_keys[1], (MODEL_WIDTH,), jnp.float32), 0.1, 1.9)
    w_query = scatter_about(arg_keys[2], (MODEL_WIDTH, QUERY_HEADS * HEAD_SIZE), (MODEL_WIDTH // 4) ** -0.5, 0.25, ((1, 2),))
    key_weight = scatter_about(arg_keys[3], (MODEL_WIDTH, KEY_VALUE_HEADS * HEAD_SIZE), MODEL_WIDTH ** -0.5, 0.125, ((1, 2),))
    value_weight = scatter_about(arg_keys[4], (MODEL_WIDTH, KEY_VALUE_HEADS * HEAD_SIZE), MODEL_WIDTH ** -0.5, 0.125, ((1, 2),))
    w_attn_out = scatter_about(arg_keys[5], (QUERY_HEADS * HEAD_SIZE, MODEL_WIDTH), (HEAD_SIZE // 4) ** -0.5, 1.0, ((0, 2),))
    kv_pages = draw_kv_pages(jax.random.fold_in(arg_keys[23], 71), 0)
    page_table = draw_page_table(jax.random.fold_in(arg_keys[23], 71), 0)
    cached_len = draw_cached_len(jax.random.fold_in(arg_keys[23], 71), 0)
    w_gate_z = scatter_about(arg_keys[9], (MODEL_WIDTH, DSSM), MODEL_WIDTH ** -0.5, 0.125, ((1, 2),))
    w_ssm_in = scatter_about(arg_keys[10], (MODEL_WIDTH, DSSM), MODEL_WIDTH ** -0.5, 0.125, ((1, 2),))
    w_bc = scatter_about(arg_keys[11], (MODEL_WIDTH, 2 * MN), MODEL_WIDTH ** -0.5, 0.125)
    w_dt = scatter_about(arg_keys[12], (MODEL_WIDTH, MH), MODEL_WIDTH ** -0.5, 0.125, ((1, 2),))
    conv_w_x = scatter_about(arg_keys[13], (KCONV, DSSM), KCONV ** -0.5, 3.0, ((1, 2),), jnp.float32)
    conv_w_bc = scatter_about(arg_keys[14], (KCONV, 2 * MN), KCONV ** -0.5, 3.0, (), jnp.float32)
    conv_x_state = scatter_about(arg_keys[15], (REQS, KCONV - 1, DSSM), 1.0, 6.0, ((0, 64), (2, 2)))
    conv_bc_state = scatter_about(arg_keys[16], (REQS, KCONV - 1, 2 * MN), 1.0, 6.0, ((0, 64),))
    dt_bias = jnp.clip(-3.0 + 3.0 * jax.random.uniform(arg_keys[17], (MH,), jnp.float32) ** level_of(arg_keys[17], (MH,), ((0, 2),), -0.2, 0.2), -3.0, 0.0)
    decay_rate = jnp.clip(jnp.exp(math.log(0.2) - 4.6051702 * jax.random.uniform(arg_keys[18], (MH,), jnp.float32) ** level_of(arg_keys[18], (MH,), ((0, 2),), -0.2, 0.2)), 0.002, 0.2)
    skip_gain = jnp.clip(0.5 + 1.0 * jax.random.uniform(arg_keys[19], (MH,), jnp.float32) ** level_of(arg_keys[19], (MH,), ((0, 2),), -0.2, 0.2), 0.5, 1.5)
    mixer_gain = jnp.clip(1.0 + 0.18 * jax.random.normal(arg_keys[20], (DSSM,), jnp.float32), 0.1, 1.9)
    w_mixer_out = scatter_about(arg_keys[21], (DSSM, MODEL_WIDTH), DSSM ** -0.5, 0.15625, ((0, 2),))
    ssm_state = scatter_about(arg_keys[22], (REQS, MH, MP, MN), 1.0, 6.0, ((0, 64), (1, 2)), jnp.float32)
    return dict(tokens=tokens, attn_gain=attn_gain, w_query=w_query, key_weight=key_weight, value_weight=value_weight, w_attn_out=w_attn_out, kv_pages=kv_pages, page_table=page_table, cached_len=cached_len, w_gate_z=w_gate_z, w_ssm_in=w_ssm_in, w_bc=w_bc, w_dt=w_dt, conv_w_x=conv_w_x, conv_w_bc=conv_w_bc, conv_x_state=conv_x_state, conv_bc_state=conv_bc_state, dt_bias=dt_bias, decay_rate=decay_rate, skip_gain=skip_gain, mixer_gain=mixer_gain, w_mixer_out=w_mixer_out, ssm_state=ssm_state)


EPSILON = 1e-05
ROPE_BASE = 100000.0
NEG_FILL = -1e+30

def rms_scale(value_vectors, gain_row):
    mean_sq = lax.optimization_barrier(jnp.mean(value_vectors * value_vectors, axis=-1, keepdims=True))
    return value_vectors * lax.rsqrt(mean_sq + EPSILON) * gain_row

def stored(value_vectors):
    return lax.optimization_barrier(value_vectors.astype(jnp.bfloat16))

def apply_rotary(value_vectors, token_positions):
    full_width = value_vectors.shape[-1]
    half_width = full_width // 2
    inverse = ROPE_BASE ** (-2.0 * jnp.arange(half_width, dtype=jnp.float32) / full_width)
    angles = token_positions.astype(jnp.float32)[:, None] * inverse[None, :]
    cosine = jnp.concatenate([jnp.cos(angles), jnp.cos(angles)], axis=-1)[:, None, :]
    sine_row = jnp.concatenate([jnp.sin(angles), jnp.sin(angles)], axis=-1)[:, None, :]
    turned = jnp.concatenate([-value_vectors[..., half_width:], value_vectors[..., :half_width]], axis=-1)
    return value_vectors * cosine + turned * sine_row

def short_conv(history, fresh_rows, kernel):
    joined = jnp.concatenate([history, fresh_rows], axis=0).astype(jnp.float32)
    row_count = fresh_rows.shape[0]
    summed = joined[0:row_count] * kernel[0]
    for tap_index in range(1, kernel.shape[0]):
        summed = summed + joined[tap_index:tap_index + row_count] * kernel[tap_index]
    return jax.nn.silu(summed)

def ssm_block(ssm_x, step_size, decay_rate, b_vectors, c_vectors, state_in, skip_gain):
    row_count = ssm_x.shape[0]
    row_order = jnp.arange(row_count, dtype=jnp.int32)
    causal = row_order[None, :] <= row_order[:, None]
    cumulative = jnp.cumsum(-step_size * decay_rate, axis=0)
    gap = cumulative.T[:, :, None] - cumulative.T[:, None, :]
    inner = jnp.dot(c_vectors.astype(jnp.float32), b_vectors.astype(jnp.float32).T, precision=lax.Precision.HIGHEST)
    mixing = stored(jnp.where(causal[None], jnp.exp(jnp.minimum(gap, 0.0)), 0.0) * inner[None])
    x_float = ssm_x.astype(jnp.float32)
    moved_float = x_float * step_size[:, :, None]
    moved = stored(moved_float)
    intra = jnp.einsum('hij,jhp->ihp', mixing.astype(jnp.float32), moved.astype(jnp.float32), precision=lax.Precision.HIGHEST)
    carried = jnp.exp(cumulative)[:, :, None] * jnp.einsum('in,hpn->ihp', c_vectors.astype(jnp.float32), state_in, precision=lax.Precision.HIGHEST)
    ssm_y = intra + carried + skip_gain[None, :, None] * x_float
    tail_fade = jnp.exp(cumulative[-1][None, :] - cumulative)
    tail_moved = stored(moved_float * tail_fade[:, :, None])
    last_state = jnp.exp(cumulative[-1])[:, None, None] * state_in + jnp.einsum('jhp,jn->hpn', tail_moved.astype(jnp.float32), b_vectors.astype(jnp.float32), precision=lax.Precision.HIGHEST)
    return (ssm_y, last_state)

def reference(tokens, attn_gain, w_query, key_weight, value_weight, w_attn_out, kv_pages, page_table, cached_len, w_gate_z, w_ssm_in, w_bc, w_dt, conv_w_x, conv_w_bc, conv_x_state, conv_bc_state, dt_bias, decay_rate, skip_gain, mixer_gain, w_mixer_out, ssm_state):
    queries_per_group = QUERY_HEADS // KEY_VALUE_HEADS
    score_scale = 1.0 / math.sqrt(HEAD_SIZE)

    def one_request(inputs):
        request_tokens, table_row, length, history_x, history_bc, state_in = inputs
        normed_input = rms_scale(request_tokens.astype(jnp.float32), attn_gain).astype(jnp.bfloat16)
        token_positions = length + jnp.arange(NEW_TOKENS, dtype=jnp.int32)
        query_vectors = apply_rotary(jnp.dot(normed_input, w_query, preferred_element_type=jnp.float32).reshape(NEW_TOKENS, QUERY_HEADS, HEAD_SIZE), token_positions).astype(jnp.bfloat16)
        incoming_keys = apply_rotary(jnp.dot(normed_input, key_weight, preferred_element_type=jnp.float32).reshape(NEW_TOKENS, KEY_VALUE_HEADS, HEAD_SIZE), token_positions).astype(jnp.bfloat16)
        incoming_values = jnp.dot(normed_input, value_weight, preferred_element_type=jnp.float32).astype(jnp.bfloat16).reshape(NEW_TOKENS, KEY_VALUE_HEADS, HEAD_SIZE)
        page_table_rows = kv_pages[table_row]
        cached_key_rows = jnp.transpose(page_table_rows[:, 0], (1, 0, 2, 3)).reshape(KEY_VALUE_HEADS, TABLE_ENTRIES * PAGE_TOKENS, HEAD_SIZE)
        cached_value_rows = jnp.transpose(page_table_rows[:, 1], (1, 0, 2, 3)).reshape(KEY_VALUE_HEADS, TABLE_ENTRIES * PAGE_TOKENS, HEAD_SIZE)
        all_keys = jnp.concatenate([cached_key_rows, jnp.transpose(incoming_keys, (1, 0, 2))], axis=1).astype(jnp.float32)
        all_vals = jnp.concatenate([cached_value_rows, jnp.transpose(incoming_values, (1, 0, 2))], axis=1).astype(jnp.float32)
        cache_slots = jnp.arange(TABLE_ENTRIES * PAGE_TOKENS, dtype=jnp.int32)
        row_order = jnp.arange(NEW_TOKENS, dtype=jnp.int32)
        visible = jnp.concatenate([jnp.broadcast_to(cache_slots[None, :] < length, (NEW_TOKENS, TABLE_ENTRIES * PAGE_TOKENS)), row_order[None, :] <= row_order[:, None]], axis=1)
        query_groups = query_vectors.reshape(NEW_TOKENS, KEY_VALUE_HEADS, queries_per_group, HEAD_SIZE).astype(jnp.float32)
        scores = jnp.einsum('nhgd,hkd->hgnk', query_groups, all_keys) * score_scale
        scores = jnp.where(visible, scores, NEG_FILL)
        row_top = lax.optimization_barrier(jnp.max(scores, axis=-1, keepdims=True))
        weights = jnp.where(visible, jnp.exp(scores - row_top), 0.0)
        weight_sum = lax.optimization_barrier(jnp.sum(weights, axis=-1, keepdims=True))
        rounded = lax.optimization_barrier(weights.astype(jnp.bfloat16)).astype(jnp.float32)
        context = jnp.einsum('hgnk,hkd->hgnd', rounded, all_vals) / weight_sum
        context = jnp.transpose(context, (2, 0, 1, 3)).reshape(NEW_TOKENS, QUERY_HEADS * HEAD_SIZE).astype(jnp.bfloat16)
        attn_part = jnp.dot(context, w_attn_out, preferred_element_type=jnp.float32)
        gate_z = stored(jnp.dot(normed_input, w_gate_z, preferred_element_type=jnp.float32))
        ssm_in = stored(jnp.dot(normed_input, w_ssm_in, preferred_element_type=jnp.float32))
        bc_in = stored(jnp.dot(normed_input, w_bc, preferred_element_type=jnp.float32))
        step_raw = jnp.dot(normed_input, w_dt, preferred_element_type=jnp.float32)
        ssm_x = stored(short_conv(history_x, ssm_in, conv_w_x))
        bc_rows = stored(short_conv(history_bc, bc_in, conv_w_bc))
        step_size = jax.nn.softplus(step_raw + dt_bias)
        ssm_y, last_state = ssm_block(ssm_x.reshape(NEW_TOKENS, MH, MP), step_size, decay_rate, bc_rows[:, :MN], bc_rows[:, MN:], state_in, skip_gain)
        gated = ssm_y.reshape(NEW_TOKENS, DSSM) * jax.nn.silu(gate_z.astype(jnp.float32))
        normed_y = rms_scale(gated, mixer_gain).astype(jnp.bfloat16)
        ssm_part = jnp.dot(normed_y, w_mixer_out, preferred_element_type=jnp.float32)
        return ((attn_part + ssm_part).astype(jnp.bfloat16), last_state)
    mixed, final_state = lax.map(one_request, (tokens.reshape(REQS, NEW_TOKENS, MODEL_WIDTH), page_table, cached_len, conv_x_state, conv_bc_state, ssm_state))
    return (mixed.reshape(TOKENS, MODEL_WIDTH), final_state)
```

```python
import math
from functools import partial

import jax
import jax.numpy as jnp
from jax import lax
from jax.experimental import pallas as pl
from jax.experimental.pallas import tpu as pltpu
from jax.sharding import PartitionSpec as P

HEAD = 128
MP = 64
MN = 256
DSSM = 1536
EPSILON = 1e-05
ROPE_BASE = 100000.0
NEG_FILL = -1e30
T = 512
CH = 128
F32 = jnp.float32
BF16 = jnp.bfloat16
MESH = pl.DeviceIdType.MESH


def dot(a, b):
    return lax.dot_general(a, b, (((1,), (0,)), ((), ())), preferred_element_type=F32)


def dot_nt(a, b):
    return lax.dot_general(a, b, (((1,), (1,)), ((), ())), preferred_element_type=F32)


def dot_tn(a, b):
    return lax.dot_general(a, b, (((0,), (0,)), ((), ())), preferred_element_type=F32)


def sigmoid(v):
    return 1.0 / (1.0 + jnp.exp(-v))


def split3(v):
    hi = v.astype(BF16)
    rest = v - hi.astype(F32)
    mid = rest.astype(BF16)
    low = (rest - mid.astype(F32)).astype(BF16)
    return hi, mid, low


def project_kernel(
    tok, gain, cos, sin, wdt, bias, decay, convw, hist, skip, state,
    wq, wk, wv, wx, wbc, wz,
    q_out, k_out, v_out, gated, sq_out, final,
    w, normed, proj, ub, xbc, inner, cs, cumt, cumcol, stepcol, sqs, sems,
):
    hq, hx, hn = wq.shape[1], wx.shape[1], wbc.shape[1]
    offs = [0, hq, hq + HEAD]
    base = hq + 2 * HEAD
    offs += [base, base + hx, base + hx + hn]
    copies = []
    for i, (src, off) in enumerate(zip((wq, wk, wv, wx, wbc, wz), offs)):
        cp = pltpu.make_async_copy(src, w.at[:, pl.ds(off, src.shape[1])], sems.at[i])
        cp.start()
        copies.append(cp)

    def norm_rows(i, carry):
        rows = pl.ds(pl.multiple_of(i * 64, 64), 64)
        v = tok[rows, :].astype(F32)
        mean_sq = jnp.mean(v * v, axis=-1, keepdims=True)
        normed[rows, :] = (v * lax.rsqrt(mean_sq + EPSILON) * gain[...]).astype(BF16)
        return carry

    lax.fori_loop(0, T // 64, norm_rows, 0)

    step_raw = dot(normed[...], wdt[...])
    v = step_raw + bias[...]
    step = jnp.maximum(v, 0.0) + jnp.log1p(jnp.exp(-jnp.abs(v)))
    ri = lax.broadcasted_iota(jnp.int32, (T, T), 0)
    ci = lax.broadcasted_iota(jnp.int32, (T, T), 1)
    tri = jnp.where(ri >= ci, 1.0, 0.0).astype(BF16)
    hi, mid, low = split3(-step * decay[...])
    cum = dot(tri, hi) + (dot(tri, mid) + dot(tri, low))
    cumt[...] = cum.T
    heads = skip.shape[0]
    for h in range(heads):
        cumcol[h] = jnp.broadcast_to(cum[:, h : h + 1], (T, 128))
        stepcol[h] = jnp.broadcast_to(step[:, h : h + 1], (T, 128))

    def rope(u):
        return (u * cos[...] + pltpu.roll(u, HEAD // 2, 1) * sin[...]).astype(BF16)

    for i in range(3):
        copies[i].wait()
    for n in range(hq // 256):
        acc = dot(normed[...], w[:, n * 256 : (n + 1) * 256])
        for k in range(2):
            u = rope(acc[:, k * 128 : (k + 1) * 128])
            h = n * 2 + k
            for c in range(T // CH):
                q_out[c, h * CH : (h + 1) * CH, :] = u[c * CH : (c + 1) * CH]
    acc = dot(normed[...], w[:, hq : hq + 256])
    k_out[...] = rope(acc[:, :128])
    v_out[...] = acc[:, 128:].astype(BF16)

    def proj_tile(n, carry):
        o = pl.multiple_of(n * 256, 256)
        proj[:, pl.ds(o, 256)] = dot(normed[...], w[:, pl.ds(base + o, 256)]).astype(BF16)
        return carry

    copies[3].wait()
    copies[4].wait()
    nconv = (hx + hn) // 256
    lax.fori_loop(0, nconv, proj_tile, 0)

    def conv_tile(n, carry):
        cols = pl.ds(pl.multiple_of(n * 128, 128), 128)
        ub[0:8, :] = hist[:, cols]
        ub[8 : T + 8, :] = proj[:, cols].astype(F32)
        taps = convw[:, cols]
        s = ub[5 : T + 5, :] * taps[0:1]
        s = s + ub[6 : T + 6, :] * taps[1:2]
        s = s + ub[7 : T + 7, :] * taps[2:3]
        s = s + ub[8 : T + 8, :] * taps[3:4]
        xbc[:, cols] = (s * sigmoid(s)).astype(BF16)
        return carry

    lax.fori_loop(0, (hx + hn) // 128, conv_tile, 0)
    copies[5].wait()
    lax.fori_loop(nconv, nconv + hx // 256, proj_tile, 0)

    bv = xbc[:, hx : hx + MN]
    cv = xbc[:, hx + MN :]
    inner[...] = dot_nt(cv, bv)
    st = state[...].reshape(hx, MN)
    st_hi = st.astype(BF16)
    st_lo = (st - st_hi.astype(F32)).astype(BF16)
    cs[...] = dot_nt(cv, st_hi) + dot_nt(cv, st_lo)
    sqs[...] = jnp.zeros_like(sqs)
    left = lax.broadcasted_iota(jnp.int32, (T, 128), 1) < MP
    left_row = lax.broadcasted_iota(jnp.int32, (1, 128), 1) < MP
    half = T // 2
    rb_i = lax.broadcasted_iota(jnp.int32, (half, half), 0)
    rb_j = lax.broadcasted_iota(jnp.int32, (half, half), 1)
    causal = rb_j <= rb_i

    def pair(p, carry):
        cols = pl.ds(pl.multiple_of(p * 128, 128), 128)
        ha = 2 * p
        hb = ha + 1
        xp = xbc[:, cols].astype(F32)
        stp = jnp.where(left, stepcol[ha], stepcol[hb])
        cup = jnp.where(left, cumcol[ha], cumcol[hb])
        moved_f = xp * stp
        moved = moved_f.astype(BF16)
        zero = jnp.zeros_like(moved)
        ma = jnp.where(left, moved, zero)
        mb = jnp.where(left, zero, moved)
        parts = []
        for rb in range(2):
            rows = slice(rb * half, (rb + 1) * half)
            total = None
            for h, mv in ((ha, ma), (hb, mb)):
                col = cumcol[h, rows, :]
                col = jnp.concatenate([col, col], axis=1)
                for jb in range(rb + 1):
                    js = slice(jb * half, (jb + 1) * half)
                    gap = col - cumt[pl.ds(h, 1), js]
                    e = jnp.exp(jnp.minimum(gap, 0.0)) * inner[rows, js]
                    if jb == rb:
                        e = jnp.where(causal, e, 0.0)
                    d = dot(e.astype(BF16), mv[js])
                    total = d if total is None else total + d
            parts.append(total)
        intra = jnp.concatenate(parts, axis=0)
        skip_row = jnp.where(left_row, skip[ha], skip[hb])
        y = intra + jnp.exp(cup) * cs[:, cols] + skip_row * xp
        z = proj[:, pl.ds(pl.multiple_of(hx + hn + p * 128, 128), 128)].astype(F32)
        g = y * (z * sigmoid(z))
        gated[:, cols] = g
        sqs[...] = sqs[...] + g * g
        last = cup[T - 1 : T, :]
        tail = (moved_f * jnp.exp(last - cup)).astype(BF16)
        add = dot_tn(tail, bv)
        for k, h in ((0, ha), (1, hb)):
            e = jnp.exp(cumcol[h, T - 1 : T, :])
            e = jnp.concatenate([e, e], axis=1)
            final[h] = e * state[h] + add[k * MP : (k + 1) * MP]
        return carry

    lax.fori_loop(0, heads // 2, pair, 0)
    col = jnp.sum(sqs[...], axis=-1, keepdims=True)
    rows = jnp.broadcast_to(col, (T, 128)).T
    sq_out[...] = rows[0:8]


def project_call(tok, gain, cos, sin, wdt, bias, decay, convw, hist, skip, state, weights):
    heads = state.shape[0]
    hx = heads * MP
    hn = 2 * MN
    hq = weights[0].shape[1]
    width = tok.shape[1]
    total = hq + 2 * HEAD + 2 * hx + hn
    vm = pl.BlockSpec(memory_space=pltpu.VMEM)
    hbm = pl.BlockSpec(memory_space=pl.ANY)
    sm = pl.BlockSpec(memory_space=pltpu.SMEM)
    return pl.pallas_call(
        project_kernel,
        out_shape=(
            jax.ShapeDtypeStruct((T // CH, (hq // HEAD) * CH, HEAD), BF16),
            jax.ShapeDtypeStruct((T, HEAD), BF16),
            jax.ShapeDtypeStruct((T, HEAD), BF16),
            jax.ShapeDtypeStruct((T, hx), F32),
            jax.ShapeDtypeStruct((8, T), F32),
            jax.ShapeDtypeStruct((heads, MP, MN), F32),
        ),
        in_specs=[vm] * 9 + [sm, vm] + [hbm] * 6,
        out_specs=[vm] * 6,
        scratch_shapes=[
            pltpu.VMEM((width, total), BF16),
            pltpu.VMEM((T, width), BF16),
            pltpu.VMEM((T, 2 * hx + hn), BF16),
            pltpu.VMEM((T + 8, 128), F32),
            pltpu.VMEM((T, hx + hn), BF16),
            pltpu.VMEM((T, T), F32),
            pltpu.VMEM((T, hx), F32),
            pltpu.VMEM((128, T), F32),
            pltpu.VMEM((heads, T, 128), F32),
            pltpu.VMEM((heads, T, 128), F32),
            pltpu.VMEM((T, 128), F32),
            pltpu.SemaphoreType.DMA((6,)),
        ],
        compiler_params=pltpu.CompilerParams(vmem_limit_bytes=56 * 1024 * 1024),
        cost_estimate=pl.CostEstimate(
            flops=20_000_000_000, bytes_accessed=60_000_000, transcendentals=5_000_000
        ),
        name="project_mamba",
    )(tok, gain, cos, sin, wdt, bias, decay, convw, hist, skip, state, *weights)


def attend_kernel(
    owner, length, q, k_new, v_new, gated, sq, mgain, pages, wa, wm,
    out,
    kc, vc, scores, ssm, wav, wmv, ny, sq_peer, own, send, recv, ctx, sems, ssems, rsems,
):
    tp = lax.axis_index("tp")
    peer = {"tp": 1 - tp}
    cps = []
    for i, (src, dst) in enumerate(((wm, wmv), (wa, wav))):
        cp = pltpu.make_async_copy(src, dst, sems.at[i])
        cp.start()
        cps.append(cp)
    barrier = pltpu.get_barrier_semaphore()
    pl.semaphore_signal(barrier, inc=1, device_id=peer, device_id_type=MESH)
    pl.semaphore_wait(barrier, 1)
    sq_copy = pltpu.make_async_remote_copy(
        src_ref=sq, dst_ref=sq_peer, send_sem=ssems.at[4], recv_sem=rsems.at[4],
        device_id=peer, device_id_type=MESH,
    )
    sq_copy.start()
    npages = owner.shape[0]

    def compact(i, carry):
        o = owner[i]
        rows = pl.ds(pl.multiple_of(i * 128, 128), 128)
        kc[rows, :] = pages[o, 0]
        vc[rows, :] = pages[o, 1]
        return carry

    lax.fori_loop(0, npages, compact, 0)
    cached = npages * 128
    kc[cached : cached + T, :] = k_new[...]
    vc[cached : cached + T, :] = v_new[...]
    sq_copy.wait()
    half = own.shape[1]
    hx = gated.shape[1]
    inv = lax.rsqrt((sq[0:1, :] + sq_peer[0:1, :]) * (1.0 / DSSM) + EPSILON)
    col = jnp.broadcast_to(inv, (128, T)).T

    def norm_tile(n, carry):
        cols = pl.ds(pl.multiple_of(n * 128, 128), 128)
        ny[:, cols] = (gated[:, cols] * col * mgain[:, cols]).astype(BF16)
        return carry

    lax.fori_loop(0, hx // 128, norm_tile, 0)
    cps[0].wait()

    def ssm_tile(n, carry):
        cols = pl.ds(pl.multiple_of(n * 256, 256), 256)
        ssm[:, cols] = dot(ny[...], wmv[:, cols])
        return carry

    lax.fori_loop(0, ssm.shape[1] // 256, ssm_tile, 0)
    cps[1].wait()
    heads = q.shape[1] // CH
    m_rows = heads * CH
    factor = 1.0 / math.sqrt(HEAD) * math.log2(math.e)
    kb = 512
    nblk = cached // kb
    safe = (cached * 3 // 4) // kb
    rows_i = lax.broadcasted_iota(jnp.int32, (m_rows, T), 0)
    cols_j = lax.broadcasted_iota(jnp.int32, (m_rows, T), 1)
    row_in = lax.rem(rows_i, CH)
    send_off = pl.multiple_of((1 - tp) * half, half)
    own_off = pl.multiple_of(tp * half, half)
    limit = length[0]

    def chunk_copy(c):
        return pltpu.make_async_remote_copy(
            src_ref=send.at[c], dst_ref=recv.at[c], send_sem=ssems.at[c], recv_sem=rsems.at[c],
            device_id=peer, device_id_type=MESH,
        )

    def chunk(c, carry):
        qc = q[c]
        top = jnp.full((m_rows, 128), NEG_FILL, F32)
        for b in range(nblk + 1):
            cols = slice(b * kb, (b + 1) * kb)
            s = dot_nt(qc, kc[cols, :])
            if b == nblk:
                s = jnp.where(cols_j <= row_in + c * CH, s, NEG_FILL)
            elif b >= safe:
                s = jnp.where(cols_j < limit - b * kb, s, NEG_FILL)
            scores[:, cols] = s
            for t in range(kb // 128):
                top = jnp.maximum(top, s[:, t * 128 : (t + 1) * 128])
        m = jnp.max(top, axis=-1, keepdims=True) * factor
        total = jnp.zeros((m_rows, 128), F32)
        acc = jnp.zeros((m_rows, HEAD), F32)
        for b in range(nblk + 1):
            cols = slice(b * kb, (b + 1) * kb)
            p = jnp.exp2(scores[:, cols] * factor - m)
            for t in range(kb // 128):
                total = total + p[:, t * 128 : (t + 1) * 128]
            acc = acc + dot(p.astype(BF16), vc[cols, :])
        res = (acc / jnp.sum(total, axis=-1, keepdims=True)).astype(BF16)
        for h in range(heads):
            ctx[:, h * HEAD : (h + 1) * HEAD] = res[h * CH : (h + 1) * CH]
        rows = pl.ds(pl.multiple_of(c * CH, CH), CH)
        cx = ctx[...]
        send[c] = (
            dot(cx, wav[:, pl.ds(send_off, half)]) + ssm[rows, pl.ds(send_off, half)]
        ).astype(BF16)
        own[rows, :] = dot(cx, wav[:, pl.ds(own_off, half)]) + ssm[rows, pl.ds(own_off, half)]
        chunk_copy(c).start()
        return carry

    lax.fori_loop(0, T // CH, chunk, 0)

    def finish(c, carry):
        rows = pl.ds(pl.multiple_of(c * CH, CH), CH)
        chunk_copy(c).wait()
        out[rows, :] = (own[rows, :] + recv[c].astype(F32)).astype(BF16)
        return carry

    lax.fori_loop(0, T // CH, finish, 0)


def attend_call(owner, length, q, k_new, v_new, gated, sq, mgain, pages, wa, wm):
    width = wa.shape[1]
    half = width // 2
    keys = owner.shape[0] * 128 + T
    chunks = T // CH
    hx = gated.shape[1]
    vm = pl.BlockSpec(memory_space=pltpu.VMEM)
    hbm = pl.BlockSpec(memory_space=pl.ANY)
    sm = pl.BlockSpec(memory_space=pltpu.SMEM)
    return pl.pallas_call(
        attend_kernel,
        out_shape=jax.ShapeDtypeStruct((T, half), BF16),
        in_specs=[sm, sm] + [vm] * 7 + [hbm, hbm],
        out_specs=vm,
        scratch_shapes=[
            pltpu.VMEM((keys, HEAD), BF16),
            pltpu.VMEM((keys, HEAD), BF16),
            pltpu.VMEM((q.shape[1], keys), F32),
            pltpu.VMEM((T, width), F32),
            pltpu.VMEM(wa.shape, BF16),
            pltpu.VMEM(wm.shape, BF16),
            pltpu.VMEM((T, hx), BF16),
            pltpu.VMEM((8, T), F32),
            pltpu.VMEM((T, half), F32),
            pltpu.VMEM((chunks, CH, half), BF16),
            pltpu.VMEM((chunks, CH, half), BF16),
            pltpu.VMEM((CH, wa.shape[0]), BF16),
            pltpu.SemaphoreType.DMA((2,)),
            pltpu.SemaphoreType.DMA((chunks + 1,)),
            pltpu.SemaphoreType.DMA((chunks + 1,)),
        ],
        compiler_params=pltpu.CompilerParams(
            collective_id=0, has_side_effects=True, vmem_limit_bytes=58 * 1024 * 1024
        ),
        name="attend_out",
    )(owner, length, q, k_new, v_new, gated, sq, mgain, pages, wa, wm)


def shards(
    tokens, attn_gain, w_query, key_weight, value_weight, w_attn_out, kv_pages, page_table,
    cached_len, w_gate_z, w_ssm_in, w_bc, w_dt, conv_w_x, conv_w_bc, conv_x_state, conv_bc_state,
    dt_bias, decay_rate, skip_gain, mixer_gain, w_mixer_out, ssm_state,
):
    devices = lax.axis_size("req")
    pages_dev = kv_pages.shape[0]
    row = page_table[0]
    owner = row // pages_dev
    slot = row % pages_dev
    targets = jnp.arange(devices, dtype=jnp.int32)
    want = jnp.sum(jnp.where(owner[None, :] == targets[:, None], slot[None, :], 0), axis=1)
    gathered = lax.all_gather(tokens, "tp", axis=1, tiled=True)
    requested = lax.all_to_all(want, "req", split_axis=0, concat_axis=0, tiled=True)
    fetched = kv_pages[:, :, 0][requested]
    arrived = lax.all_to_all(fetched, "req", split_axis=0, concat_axis=0, tiled=True)

    half = HEAD // 2
    inverse = ROPE_BASE ** (-2.0 * jnp.arange(half, dtype=F32) / HEAD)
    positions = cached_len[0] + jnp.arange(T, dtype=jnp.int32)
    angles = positions.astype(F32)[:, None] * inverse[None, :]
    c, s = jnp.cos(angles), jnp.sin(angles)
    cos = jnp.concatenate([c, c], axis=-1)
    sin = jnp.concatenate([-s, s], axis=-1)
    heads = w_dt.shape[1]
    wdt = jnp.pad(w_dt, ((0, 0), (0, 128 - heads)))
    bias = jnp.pad(dt_bias, (0, 128 - heads))[None]
    decay = jnp.pad(decay_rate, (0, 128 - heads))[None]
    convw = jnp.concatenate([conv_w_x, conv_w_bc], axis=1)
    hist = jnp.concatenate([conv_x_state[0], conv_bc_state[0]], axis=1).astype(F32)
    hist = jnp.pad(hist, ((5, 0), (0, 0)))
    q, k_new, v_new, gated, sq, final = project_call(
        gathered, attn_gain[None], cos, sin, wdt, bias, decay, convw, hist, skip_gain,
        ssm_state[0], (w_query, key_weight, value_weight, w_ssm_in, w_bc, w_gate_z),
    )
    mixed = attend_call(
        owner, cached_len, q, k_new, v_new, gated, sq, mixer_gain[None], arrived,
        w_attn_out, w_mixer_out,
    )
    return (mixed, final[None])


def solution(mesh):
    return jax.shard_map(
        shards,
        mesh=mesh,
        in_specs=(
            P("req", "tp"), P(), P(None, "tp"), P(None, "tp"), P(None, "tp"), P("tp", None),
            P("req", None, "tp", None, None), P("req", None), P("req"), P(None, "tp"),
            P(None, "tp"), P(), P(None, "tp"), P(None, "tp"), P(), P("req", None, "tp"),
            P("req", None, None), P("tp"), P("tp"), P("tp"), P("tp"), P("tp", None),
            P("req", "tp", None, None),
        ),
        out_specs=(P("req", "tp"), P("req", "tp", None, None)),
        check_vma=False,
    )
```

```python
import math
from functools import partial

import jax
import jax.numpy as jnp
from jax import lax
from jax.experimental import pallas as pl
from jax.experimental.pallas import tpu as pltpu
from jax.sharding import PartitionSpec as P

HEAD = 128
MP = 64
MN = 256
DSSM = 1536
EPSILON = 1e-05
ROPE_BASE = 100000.0
NEG_FILL = -1e30
T = 512
CH = 128
F32 = jnp.float32
BF16 = jnp.bfloat16
MESH = pl.DeviceIdType.MESH


def dot(a, b):
    return lax.dot_general(a, b, (((1,), (0,)), ((), ())), preferred_element_type=F32)


def dot_nt(a, b):
    return lax.dot_general(a, b, (((1,), (1,)), ((), ())), preferred_element_type=F32)


def dot_tn(a, b):
    return lax.dot_general(a, b, (((0,), (0,)), ((), ())), preferred_element_type=F32)


def sigmoid(v):
    return 1.0 / (1.0 + jnp.exp(-v))


def split3(v):
    hi = v.astype(BF16)
    rest = v - hi.astype(F32)
    mid = rest.astype(BF16)
    low = (rest - mid.astype(F32)).astype(BF16)
    return hi, mid, low


def project_kernel(
    table, tok, length, gain, bias, decay, skip, wdt, convx, convbc, histx, histbc, state,
    pages, wq, wk, wv, wx, wbc, wz,
    q_out, k_out, v_out, gated, sq_out, final, kc, vc,
    w, tokf, normed, proj, ub, xbc, inner, cs, cumt, cumcol, stepcol, sqs, wdtv, cos, sin,
    want, wants, wants_sm, kvl, sendbuf, arr,
    sems, tsend, trecv, wsend, wrecv, psend, precv,
):
    me = lax.axis_index("req")
    tp = lax.axis_index("tp")
    ndev = kvl.shape[0] if kvl.shape[0] == wants.shape[0] else wants.shape[0]
    hq, hx, hn = wq.shape[1], wx.shape[1], wbc.shape[1]
    half = tok.shape[1]
    heads = skip.shape[0]
    base = hq + 2 * HEAD
    offs = [0, hq, hq + HEAD, base, base + hx, base + hx + hn]
    kv_copy = pltpu.make_async_copy(pages.at[:, :, 0], kvl, sems.at[6])
    kv_copy.start()
    copies = []
    for i, (src, off) in enumerate(zip((wq, wk, wv, wx, wbc, wz), offs)):
        cp = pltpu.make_async_copy(src, w.at[:, pl.ds(off, src.shape[1])], sems.at[i])
        cp.start()
        copies.append(cp)
    tok_own = pltpu.make_async_copy(tok, tokf.at[tp], sems.at[7])
    tok_own.start()

    barrier = pltpu.get_barrier_semaphore()

    def greet(i, carry):
        pl.semaphore_signal(
            barrier, inc=1, device_id={"req": lax.rem(me + i, ndev)}, device_id_type=MESH
        )
        return carry

    pl.semaphore_signal(barrier, inc=1, device_id={"tp": 1 - tp}, device_id_type=MESH)
    lax.fori_loop(1, ndev, greet, 0)

    per_dev = kvl.shape[0]
    npages = table.shape[1]
    lanes = lax.broadcasted_iota(jnp.int32, want.shape, 1)
    row = jnp.zeros(want.shape, jnp.int32)
    for p in range(npages):
        entry = table[0, p]
        hit = lanes == lax.div(entry, per_dev)
        row = jnp.where(hit, lax.rem(entry, per_dev), row)
    want[...] = row
    wants[pl.ds(me, 1)] = row[None]
    pl.semaphore_wait(barrier, ndev)

    def tok_copy(c):
        rows = pl.ds(pl.multiple_of(c * CH, CH), CH)
        return pltpu.make_async_remote_copy(
            src_ref=tok.at[rows, :], dst_ref=tokf.at[tp, rows, :],
            send_sem=tsend.at[c], recv_sem=trecv.at[c],
            device_id={"tp": 1 - tp}, device_id_type=MESH,
        )

    def want_copy(i, slot, target):
        return pltpu.make_async_remote_copy(
            src_ref=want, dst_ref=wants.at[slot], send_sem=wsend.at[i], recv_sem=wrecv.at[slot],
            device_id={"req": target}, device_id_type=MESH,
        )

    def want_start(i, carry):
        want_copy(i, me, lax.rem(me + i, ndev)).start()
        return carry

    lax.fori_loop(1, ndev, want_start, 0)
    for c in range(T // CH):
        tok_copy(c).start()

    def want_wait(i, carry):
        o = lax.rem(me + i, ndev)
        cp = want_copy(i, o, o)
        cp.wait_send()
        cp.wait_recv()
        return carry

    lax.fori_loop(1, ndev, want_wait, 0)
    to_smem = pltpu.make_async_copy(wants, wants_sm, sems.at[8])
    to_smem.start()
    to_smem.wait()
    kv_copy.wait()

    def reader(t):
        y = lax.rem(me // 16 + (t // 8) % 4, 4)
        zh = lax.rem((me // 8) % 2 + t // 32, 2)
        x = lax.rem((me // 2) % 4 + (t // 2) % 4, 4)
        c = lax.rem(me % 2 + t % 2, 2)
        return ((y * 2 + zh) * 4 + x) * 2 + c

    def page_copy(t, slot, target):
        return pltpu.make_async_remote_copy(
            src_ref=sendbuf.at[t], dst_ref=arr.at[slot], send_sem=psend.at[t],
            recv_sem=precv.at[slot], device_id={"req": target}, device_id_type=MESH,
        )

    arr[pl.ds(me, 1)] = kvl[pl.ds(wants_sm[me, 0, me], 1)]

    def page_pack(t, carry):
        sendbuf[pl.ds(t, 1)] = kvl[pl.ds(wants_sm[reader(t), 0, me], 1)]
        return carry

    def page_start(t, carry):
        page_copy(t, me, reader(t)).start()
        return carry

    lax.fori_loop(1, ndev, page_pack, 0)
    lax.fori_loop(1, ndev, page_start, 0)

    lane = lax.broadcasted_iota(jnp.int32, (T, HEAD), 1)
    freq = jnp.exp(lax.rem(lane, HEAD // 2).astype(F32) * (-2.0 * math.log(ROPE_BASE) / HEAD))
    posn = (length[0] + lax.broadcasted_iota(jnp.int32, (T, HEAD), 0)).astype(F32)
    angle = posn * freq
    cos[...] = jnp.cos(angle)
    sn = jnp.sin(angle)
    sin[...] = jnp.where(lane < HEAD // 2, -sn, sn)
    wdtv[...] = jnp.zeros_like(wdtv)
    wdtv[0:heads, :] = wdt[...]
    head_lane = lax.broadcasted_iota(jnp.int32, (1, 128), 1)
    bias_row = jnp.zeros((1, 128), F32)
    decay_row = jnp.zeros((1, 128), F32)
    for h in range(heads):
        bias_row = jnp.where(head_lane == h, bias[h], bias_row)
        decay_row = jnp.where(head_lane == h, decay[h], decay_row)

    tok_own.wait()
    for c in range(T // CH):
        cp = pltpu.make_async_remote_copy(
            src_ref=tok.at[c * CH : (c + 1) * CH, :],
            dst_ref=tokf.at[1 - tp, c * CH : (c + 1) * CH, :],
            send_sem=tsend.at[c], recv_sem=trecv.at[c],
            device_id={"tp": 1 - tp}, device_id_type=MESH,
        )
        cp.wait_recv()

        def norm_rows(i, carry):
            rows = pl.ds(pl.multiple_of(c * CH + i * 64, 64), 64)
            v0 = tokf[0, rows, :].astype(F32)
            v1 = tokf[1, rows, :].astype(F32)
            ms = jnp.sum(v0 * v0, axis=-1, keepdims=True) + jnp.sum(v1 * v1, axis=-1, keepdims=True)
            scale = lax.rsqrt(ms * (0.5 / half) + EPSILON)
            normed[rows, 0:half] = (v0 * scale * gain[:, 0:half]).astype(BF16)
            normed[rows, half:] = (v1 * scale * gain[:, half:]).astype(BF16)
            return carry

        lax.fori_loop(0, CH // 64, norm_rows, 0)

    v = dot_nt(normed[...], wdtv[...]) + bias_row
    step = jnp.maximum(v, 0.0) + jnp.log1p(jnp.exp(-jnp.abs(v)))
    ri = lax.broadcasted_iota(jnp.int32, (T, T), 0)
    ci = lax.broadcasted_iota(jnp.int32, (T, T), 1)
    tri = jnp.where(ri >= ci, 1.0, 0.0).astype(BF16)
    hi, mid, low = split3(-step * decay_row)
    cum = dot(tri, hi) + (dot(tri, mid) + dot(tri, low))
    cumt[...] = cum.T
    for h in range(heads):
        cumcol[h] = jnp.broadcast_to(cum[:, h : h + 1], (T, 128))
        stepcol[h] = jnp.broadcast_to(step[:, h : h + 1], (T, 128))

    def rope(u):
        return (u * cos[...] + pltpu.roll(u, HEAD // 2, 1) * sin[...]).astype(BF16)

    for i in range(3):
        copies[i].wait()
    for n in range(hq // 256):
        acc = dot(normed[...], w[:, n * 256 : (n + 1) * 256])
        for k in range(2):
            u = rope(acc[:, k * 128 : (k + 1) * 128])
            h = n * 2 + k
            for c in range(T // CH):
                q_out[c, h * CH : (h + 1) * CH, :] = u[c * CH : (c + 1) * CH]
    acc = dot(normed[...], w[:, hq : hq + 256])
    k_out[...] = rope(acc[:, :128])
    v_out[...] = acc[:, 128:].astype(BF16)

    def proj_tile(n, carry):
        o = pl.multiple_of(n * 256, 256)
        proj[:, pl.ds(o, 256)] = dot(normed[...], w[:, pl.ds(base + o, 256)]).astype(BF16)
        return carry

    copies[3].wait()
    copies[4].wait()
    nconv = (hx + hn) // 256
    lax.fori_loop(0, nconv, proj_tile, 0)

    def conv_tile(n, carry, hist, convw, start):
        local = pl.ds(pl.multiple_of(n * 128, 128), 128)
        cols = pl.ds(pl.multiple_of(start + n * 128, 128), 128)
        ub[5:8, :] = hist[:, local].astype(F32)
        ub[8 : T + 8, :] = proj[:, cols].astype(F32)
        taps = convw[:, local]
        s = ub[5 : T + 5, :] * taps[0:1]
        s = s + ub[6 : T + 6, :] * taps[1:2]
        s = s + ub[7 : T + 7, :] * taps[2:3]
        s = s + ub[8 : T + 8, :] * taps[3:4]
        xbc[:, cols] = (s * sigmoid(s)).astype(BF16)
        return carry

    lax.fori_loop(0, hx // 128, partial(conv_tile, hist=histx, convw=convx, start=0), 0)
    lax.fori_loop(0, hn // 128, partial(conv_tile, hist=histbc, convw=convbc, start=hx), 0)
    copies[5].wait()
    lax.fori_loop(nconv, nconv + hx // 256, proj_tile, 0)

    bv = xbc[:, hx : hx + MN]
    cv = xbc[:, hx + MN :]
    inner[...] = dot_nt(cv, bv)
    st = state[...].reshape(hx, MN)
    st_hi = st.astype(BF16)
    st_lo = (st - st_hi.astype(F32)).astype(BF16)
    cs[...] = dot_nt(cv, st_hi) + dot_nt(cv, st_lo)
    sqs[...] = jnp.zeros_like(sqs)
    left = lax.broadcasted_iota(jnp.int32, (T, 128), 1) < MP
    left_row = lax.broadcasted_iota(jnp.int32, (1, 128), 1) < MP
    half = T // 2
    rb_i = lax.broadcasted_iota(jnp.int32, (half, half), 0)
    rb_j = lax.broadcasted_iota(jnp.int32, (half, half), 1)
    causal = rb_j <= rb_i

    def pair(p, carry):
        cols = pl.ds(pl.multiple_of(p * 128, 128), 128)
        ha = 2 * p
        hb = ha + 1
        xp = xbc[:, cols].astype(F32)
        stp = jnp.where(left, stepcol[ha], stepcol[hb])
        cup = jnp.where(left, cumcol[ha], cumcol[hb])
        moved_f = xp * stp
        moved = moved_f.astype(BF16)
        zero = jnp.zeros_like(moved)
        ma = jnp.where(left, moved, zero)
        mb = jnp.where(left, zero, moved)
        parts = []
        for rb in range(2):
            rows = slice(rb * half, (rb + 1) * half)
            total = None
            for h, mv in ((ha, ma), (hb, mb)):
                col = cumcol[h, rows, :]
                col = jnp.concatenate([col, col], axis=1)
                for jb in range(rb + 1):
                    js = slice(jb * half, (jb + 1) * half)
                    gap = col - cumt[pl.ds(h, 1), js]
                    e = jnp.exp(jnp.minimum(gap, 0.0)) * inner[rows, js]
                    if jb == rb:
                        e = jnp.where(causal, e, 0.0)
                    d = dot(e.astype(BF16), mv[js])
                    total = d if total is None else total + d
            parts.append(total)
        intra = jnp.concatenate(parts, axis=0)
        skip_row = jnp.where(left_row, skip[ha], skip[hb])
        y = intra + jnp.exp(cup) * cs[:, cols] + skip_row * xp
        z = proj[:, pl.ds(pl.multiple_of(hx + hn + p * 128, 128), 128)].astype(F32)
        g = y * (z * sigmoid(z))
        gated[:, cols] = g
        sqs[...] = sqs[...] + g * g
        last = cup[T - 1 : T, :]
        tail = (moved_f * jnp.exp(last - cup)).astype(BF16)
        add = dot_tn(tail, bv)
        for k, h in ((0, ha), (1, hb)):
            e = jnp.exp(cumcol[h, T - 1 : T, :])
            e = jnp.concatenate([e, e], axis=1)
            final[h] = e * state[h] + add[k * MP : (k + 1) * MP]
        return carry

    lax.fori_loop(0, heads // 2, pair, 0)
    col = jnp.sum(sqs[...], axis=-1, keepdims=True)
    rows = jnp.broadcast_to(col, (T, 128)).T
    sq_out[...] = rows[0:8]

    def page_wait(t, carry):
        o = reader(t)
        cp = page_copy(t, o, o)
        cp.wait_recv()
        cp.wait_send()
        return carry

    lax.fori_loop(1, ndev, page_wait, 0)

    def compact(i, carry):
        o = lax.div(table[0, i], per_dev)
        rows = pl.ds(pl.multiple_of(i * 128, 128), 128)
        kc[rows, :] = arr[o, 0]
        vc[rows, :] = arr[o, 1]
        return carry

    lax.fori_loop(0, npages, compact, 0)
    for c in range(T // CH):
        tok_copy(c).wait_send()


def project_call(ndev, table, tok, length, gain, bias, decay, skip, wdt, convx, convbc, histx, histbc,
                 state, pages, weights):
    heads = state.shape[0]
    hx = heads * MP
    hn = 2 * MN
    hq = weights[0].shape[1]
    half = tok.shape[1]
    width = 2 * half
    total = hq + 2 * HEAD + 2 * hx + hn
    cached = table.shape[1] * 128
    per_dev = pages.shape[0]
    vm = pl.BlockSpec(memory_space=pltpu.VMEM)
    hbm = pl.BlockSpec(memory_space=pl.ANY)
    sm = pl.BlockSpec(memory_space=pltpu.SMEM)
    dma = pltpu.SemaphoreType.DMA
    return pl.pallas_call(
        project_kernel,
        out_shape=(
            jax.ShapeDtypeStruct((T // CH, (hq // HEAD) * CH, HEAD), BF16),
            jax.ShapeDtypeStruct((T, HEAD), BF16),
            jax.ShapeDtypeStruct((T, HEAD), BF16),
            jax.ShapeDtypeStruct((T, hx), F32),
            jax.ShapeDtypeStruct((8, T), F32),
            jax.ShapeDtypeStruct((heads, MP, MN), F32),
            jax.ShapeDtypeStruct((cached, HEAD), BF16),
            jax.ShapeDtypeStruct((cached, HEAD), BF16),
        ),
        in_specs=[sm, vm, sm, vm, sm, sm, sm] + [vm] * 6 + [hbm] * 7,
        out_specs=[vm] * 8,
        scratch_shapes=[
            pltpu.VMEM((width, total), BF16),
            pltpu.VMEM((2, T, half), BF16),
            pltpu.VMEM((T, width), BF16),
            pltpu.VMEM((T, 2 * hx + hn), BF16),
            pltpu.VMEM((T + 8, 128), F32),
            pltpu.VMEM((T, hx + hn), BF16),
            pltpu.VMEM((T, T), F32),
            pltpu.VMEM((T, hx), F32),
            pltpu.VMEM((128, T), F32),
            pltpu.VMEM((heads, T, 128), F32),
            pltpu.VMEM((heads, T, 128), F32),
            pltpu.VMEM((T, 128), F32),
            pltpu.VMEM((128, width), BF16),
            pltpu.VMEM((T, HEAD), F32),
            pltpu.VMEM((T, HEAD), F32),
            pltpu.VMEM((1, 128), jnp.int32),
            pltpu.VMEM((ndev, 1, 128), jnp.int32),
            pltpu.SMEM((ndev, 1, 128), jnp.int32),
            pltpu.VMEM((per_dev, 2, 128, HEAD), BF16),
            pltpu.VMEM((ndev, 2, 128, HEAD), BF16),
            pltpu.VMEM((ndev, 2, 128, HEAD), BF16),
            dma((9,)),
            dma((T // CH,)),
            dma((T // CH,)),
            dma((ndev,)),
            dma((ndev,)),
            dma((ndev,)),
            dma((ndev,)),
        ],
        compiler_params=pltpu.CompilerParams(
            collective_id=1, has_side_effects=True, vmem_limit_bytes=63 * 1024 * 1024
        ),
        name="gather_project",
    )(table, tok, length, gain, bias, decay, skip, wdt, convx, convbc, histx, histbc, state, pages, *weights)


def attend_kernel(
    length, q, k_new, v_new, gated, sq, mgain, kc_in, vc_in, wa, wm,
    out,
    kc, vc, scores, ssm, wav, wmv, ny, sq_peer, own, send, recv, ctx, sems, ssems, rsems,
):
    tp = lax.axis_index("tp")
    peer = {"tp": 1 - tp}
    cps = []
    for i, (src, dst) in enumerate(((wm, wmv), (wa, wav))):
        cp = pltpu.make_async_copy(src, dst, sems.at[i])
        cp.start()
        cps.append(cp)
    barrier = pltpu.get_barrier_semaphore()
    pl.semaphore_signal(barrier, inc=1, device_id=peer, device_id_type=MESH)
    pl.semaphore_wait(barrier, 1)
    sq_copy = pltpu.make_async_remote_copy(
        src_ref=sq, dst_ref=sq_peer, send_sem=ssems.at[4], recv_sem=rsems.at[4],
        device_id=peer, device_id_type=MESH,
    )
    sq_copy.start()
    cached = kc_in.shape[0]
    kc[0:cached, :] = kc_in[...]
    vc[0:cached, :] = vc_in[...]
    kc[cached : cached + T, :] = k_new[...]
    vc[cached : cached + T, :] = v_new[...]
    sq_copy.wait()
    half = own.shape[1]
    hx = gated.shape[1]
    inv = lax.rsqrt((sq[0:1, :] + sq_peer[0:1, :]) * (1.0 / DSSM) + EPSILON)
    col = jnp.broadcast_to(inv, (128, T)).T

    def norm_tile(n, carry):
        cols = pl.ds(pl.multiple_of(n * 128, 128), 128)
        ny[:, cols] = (gated[:, cols] * col * mgain[:, cols]).astype(BF16)
        return carry

    lax.fori_loop(0, hx // 128, norm_tile, 0)
    cps[0].wait()

    def ssm_tile(n, carry):
        cols = pl.ds(pl.multiple_of(n * 256, 256), 256)
        ssm[:, cols] = dot(ny[...], wmv[:, cols])
        return carry

    lax.fori_loop(0, ssm.shape[1] // 256, ssm_tile, 0)
    cps[1].wait()
    heads = q.shape[1] // CH
    m_rows = heads * CH
    factor = 1.0 / math.sqrt(HEAD) * math.log2(math.e)
    kb = 512
    nblk = cached // kb
    safe = (cached * 3 // 4) // kb
    rows_i = lax.broadcasted_iota(jnp.int32, (m_rows, T), 0)
    cols_j = lax.broadcasted_iota(jnp.int32, (m_rows, T), 1)
    row_in = lax.rem(rows_i, CH)
    send_off = pl.multiple_of((1 - tp) * half, half)
    own_off = pl.multiple_of(tp * half, half)
    limit = length[0]

    def chunk_copy(c):
        return pltpu.make_async_remote_copy(
            src_ref=send.at[c], dst_ref=recv.at[c], send_sem=ssems.at[c], recv_sem=rsems.at[c],
            device_id=peer, device_id_type=MESH,
        )

    def chunk(c, carry):
        qc = q[c]
        top = jnp.full((m_rows, 128), NEG_FILL, F32)
        for b in range(nblk + 1):
            cols = slice(b * kb, (b + 1) * kb)
            s = dot_nt(qc, kc[cols, :])
            if b == nblk:
                s = jnp.where(cols_j <= row_in + c * CH, s, NEG_FILL)
            elif b >= safe:
                s = jnp.where(cols_j < limit - b * kb, s, NEG_FILL)
            scores[:, cols] = s
            for t in range(kb // 128):
                top = jnp.maximum(top, s[:, t * 128 : (t + 1) * 128])
        m = jnp.max(top, axis=-1, keepdims=True) * factor
        total = jnp.zeros((m_rows, 128), F32)
        acc = jnp.zeros((m_rows, HEAD), F32)
        for b in range(nblk + 1):
            cols = slice(b * kb, (b + 1) * kb)
            p = jnp.exp2(scores[:, cols] * factor - m)
            for t in range(kb // 128):
                total = total + p[:, t * 128 : (t + 1) * 128]
            acc = acc + dot(p.astype(BF16), vc[cols, :])
        res = (acc / jnp.sum(total, axis=-1, keepdims=True)).astype(BF16)
        for h in range(heads):
            ctx[:, h * HEAD : (h + 1) * HEAD] = res[h * CH : (h + 1) * CH]
        rows = pl.ds(pl.multiple_of(c * CH, CH), CH)
        cx = ctx[...]
        send[c] = (
            dot(cx, wav[:, pl.ds(send_off, half)]) + ssm[rows, pl.ds(send_off, half)]
        ).astype(BF16)
        own[rows, :] = dot(cx, wav[:, pl.ds(own_off, half)]) + ssm[rows, pl.ds(own_off, half)]
        chunk_copy(c).start()
        return carry

    lax.fori_loop(0, T // CH, chunk, 0)

    def finish(c, carry):
        rows = pl.ds(pl.multiple_of(c * CH, CH), CH)
        chunk_copy(c).wait()
        out[rows, :] = (own[rows, :] + recv[c].astype(F32)).astype(BF16)
        return carry

    lax.fori_loop(0, T // CH, finish, 0)


def attend_call(length, q, k_new, v_new, gated, sq, mgain, kc, vc, wa, wm):
    width = wa.shape[1]
    half = width // 2
    keys = kc.shape[0] + T
    chunks = T // CH
    hx = gated.shape[1]
    vm = pl.BlockSpec(memory_space=pltpu.VMEM)
    hbm = pl.BlockSpec(memory_space=pl.ANY)
    sm = pl.BlockSpec(memory_space=pltpu.SMEM)
    return pl.pallas_call(
        attend_kernel,
        out_shape=jax.ShapeDtypeStruct((T, half), BF16),
        in_specs=[sm] + [vm] * 8 + [hbm, hbm],
        out_specs=vm,
        scratch_shapes=[
            pltpu.VMEM((keys, HEAD), BF16),
            pltpu.VMEM((keys, HEAD), BF16),
            pltpu.VMEM((q.shape[1], keys), F32),
            pltpu.VMEM((T, width), F32),
            pltpu.VMEM(wa.shape, BF16),
            pltpu.VMEM(wm.shape, BF16),
            pltpu.VMEM((T, hx), BF16),
            pltpu.VMEM((8, T), F32),
            pltpu.VMEM((T, half), F32),
            pltpu.VMEM((chunks, CH, half), BF16),
            pltpu.VMEM((chunks, CH, half), BF16),
            pltpu.VMEM((CH, wa.shape[0]), BF16),
            pltpu.SemaphoreType.DMA((2,)),
            pltpu.SemaphoreType.DMA((chunks + 1,)),
            pltpu.SemaphoreType.DMA((chunks + 1,)),
        ],
        compiler_params=pltpu.CompilerParams(
            collective_id=0, has_side_effects=True, vmem_limit_bytes=58 * 1024 * 1024
        ),
        name="attend_out",
    )(length, q, k_new, v_new, gated, sq, mgain, kc, vc, wa, wm)


def shards(
    tokens, attn_gain, w_query, key_weight, value_weight, w_attn_out, kv_pages, page_table,
    cached_len, w_gate_z, w_ssm_in, w_bc, w_dt, conv_w_x, conv_w_bc, conv_x_state, conv_bc_state,
    dt_bias, decay_rate, skip_gain, mixer_gain, w_mixer_out, ssm_state,
):
    ndev = lax.axis_size("req")
    q, k_new, v_new, gated, sq, final, kc, vc = project_call(
        ndev, page_table, tokens, cached_len, attn_gain[None], dt_bias, decay_rate, skip_gain,
        w_dt.T, conv_w_x, conv_w_bc, conv_x_state[0], conv_bc_state[0], ssm_state[0], kv_pages,
        (w_query, key_weight, value_weight, w_ssm_in, w_bc, w_gate_z),
    )
    mixed = attend_call(
        cached_len, q, k_new, v_new, gated, sq, mixer_gain[None], kc, vc, w_attn_out, w_mixer_out,
    )
    return (mixed, final[None])


def solution(mesh):
    return jax.shard_map(
        shards,
        mesh=mesh,
        in_specs=(
            P("req", "tp"), P(), P(None, "tp"), P(None, "tp"), P(None, "tp"), P("tp", None),
            P("req", None, "tp", None, None), P("req", None), P("req"), P(None, "tp"),
            P(None, "tp"), P(), P(None, "tp"), P(None, "tp"), P(), P("req", None, "tp"),
            P("req", None, None), P("tp"), P("tp"), P("tp"), P("tp"), P("tp", None),
            P("req", "tp", None, None),
        ),
        out_specs=(P("req", "tp"), P("req", "tp", None, None)),
        check_vma=False,
    )
```
